256 devices in a mesh: seq: 64 (over y, z, core), utt: 4 (over x).
Axes of the slice: x: 4, y: 4, z: 8, core: 2. Of those that a mesh axis runs over, the one named last changes fastest.
Arguments:
- features: bfloat16 [4, 16384, 1024], P('utt', 'seq'), may hold values from -6 to 6
- cotangent: bfloat16 [4, 16384, 1024], P('utt', 'seq'), may hold values from -100 to 100
- conv_kernel: float32 [31, 1024], replicated, may hold values from -1 to 1
- norm_gain: float32 [1024], replicated, may hold values from 0.25 to 1.75
- weight_in: bfloat16 [1024, 4096], P('seq', 'utt'), may hold values from -0.1875 to 0.1875
- weight_out: bfloat16 [4096, 1024], P(('utt', 'seq')), may hold values from -0.09375 to 0.09375
- keep_count: int32 [4, 64], P('utt'), may hold values from 0 to 256, as said below
- keep_index: int32 [4, 16384], P('utt', 'seq'), may hold values from 0 to 255, as said below
Outputs:
- grad_features: bfloat16 [4, 16384, 1024], P('utt', 'seq')
- grad_weight_in: float32 [1024, 4096], P('seq', 'utt')
- grad_weight_out: float32 [4096, 1024], P(('utt', 'seq'))
- grad_kernel: float32 [31, 1024], replicated
- grad_gain: float32 [1024], replicated
The draws below stay inside these ranges and needn't reach their ends.
Inputs may be any that keep to these rules, and one draw needn't show every extreme that they name: keep_count[u, s] counts the kept frames of shard s (frames s * 256 to (s + 1) * 256 - 1) of utterance u. With the blocks of a shard being its count divided by 128 and rounded up, the shards before shard s hold between s * 1 and (s + 1) * 1 blocks, and the 64 shards of an utterance hold exactly 64 blocks. For shard s of utterance u, the entries keep_index[u, s * 256 + j] with j below keep_count[u, s] are distinct frame indices within the shard in rising order; the other entries are 0.
All inputs are finite; a program needn't handle non-finite values.
Results may differ from the reference program's by a relative error of at most 0.0085.
Values may be sent and summed in bfloat16 or wider, within the bound.
No kernel may reach another device: no remote copies, remote signals or barrier semaphores. Data moves between devices by JAX's collectives and lax.ppermute only.
A program may use at most 64 MiB of HBM per device.

```python
import math
import jax
import jax.numpy as jnp
from jax import lax

D = 1024
FFN_WIDTH = 4096
KERNEL = 31
BLOCK = 128
KEPT = 1
FRAMES_DEV = 256
SHARDS = 64
UTTS = 4
FRAMES = 16384


def shard_order(key):
    return jax.random.permutation(key, FRAMES_DEV)


def one_utterance(key):
    keys = jax.random.split(key, 4)
    interior = jax.random.randint(keys[0], (SHARDS - 1,), 0, KEPT + 1).astype(jnp.int32)
    zero_one = jnp.zeros((1,), jnp.int32)
    excess = jnp.concatenate([zero_one, interior, zero_one])
    forced = jax.random.randint(keys[1], (), 1, SHARDS - 1)
    position = jnp.arange(SHARDS + 1, dtype=jnp.int32)
    excess = jnp.where(position == forced, 0, excess)
    excess = jnp.where(position == forced + 1, KEPT, excess)
    excess = jnp.where(position == forced + 2, 0, excess)
    blocks = KEPT + excess[1:] - excess[:-1]
    shard_ids = jnp.arange(SHARDS, dtype=jnp.int32)
    trimmed = jax.random.randint(keys[2], (SHARDS,), 0, BLOCK // 4).astype(jnp.int32)
    trimmed = jnp.where(shard_ids == forced, 0, trimmed)
    counts = jnp.maximum(blocks * BLOCK - trimmed, 0).astype(jnp.int32)
    orders = jax.vmap(shard_order)(jax.random.split(keys[3], SHARDS)).astype(jnp.int32)
    slot = jnp.arange(FRAMES_DEV, dtype=jnp.int32)
    chosen = slot[None, :] < counts[:, None]
    scores = jnp.where(chosen, orders, FRAMES_DEV)
    ranked = jnp.sort(scores, axis=1)
    indices = jnp.where(chosen, ranked, 0).astype(jnp.int32)
    return (counts, indices.reshape(-1))


def keep_tables(key):
    base_key = jax.random.fold_in(key, 11)
    utter_keys = jax.random.split(base_key, UTTS)
    return jax.vmap(one_utterance)(utter_keys)


def draw_keep_count(key, part):
    return keep_tables(key)[0]


def draw_keep_index(key, part):
    return keep_tables(key)[1]


def draw_cotangent(key, part):
    keys = jax.random.split(key, 4)
    position = jnp.arange(FRAMES, dtype=jnp.float32)
    rising = (1.0 + 2.0 * position / (FRAMES - 1)) / 2.0
    col_scale = jnp.exp(jax.random.uniform(keys[0], (1, 1, D), minval=0.0, maxval=math.log(10.0))) / math.sqrt(10.0)
    base_values = jnp.clip(jax.random.normal(keys[1], (UTTS, FRAMES, D)), -4.0, 4.0)
    row_scale = jnp.exp(jax.random.uniform(keys[3], (UTTS, FRAMES, 1), minval=0.0, maxval=math.log(10.0))) / math.sqrt(10.0)
    values = base_values * row_scale
    return (values * rising[None, :, None] * col_scale).astype(jnp.bfloat16)


def block_scale(own_key, dims, cuts, smallest, top_value):
    loudness, own = 1.0, jax.random.fold_in(own_key, 6)
    for dim, blocks in cuts:
        heights = jnp.exp(jax.random.uniform(jax.random.fold_in(own, dim), (blocks,), jnp.float32, smallest / len(cuts), top_value / len(cuts)))
        loudness = loudness * jnp.repeat(heights, dims[dim] // blocks).reshape([-1 if axis == dim else 1 for axis in range(len(dims))])
    return loudness


def noise(own_key, dims, deviation, most, pieces=(), kind=jnp.bfloat16):
    array = jax.random.normal(own_key, dims, jnp.float32) * deviation
    if len(pieces) > 0:
        array = block_scale(own_key, dims, pieces, -0.22, 0.18) * array
    return jnp.clip(array, min=-most, max=most).astype(kind)


def setup_inputs(seed: int = 0) -> dict:
    arg_keys = jax.random.split(jax.random.key(seed), 9)
    return {
        "features": noise(arg_keys[0], (UTTS, FRAMES, D), 1.0, 6.0, ((0, 4), (1, 64))),
        "cotangent": draw_cotangent(jax.random.fold_in(arg_keys[8], 71), 0),
        "conv_kernel": noise(arg_keys[2], (KERNEL, D), KERNEL ** -0.5, 1.0, (), jnp.float32),
        "norm_gain": jnp.clip(1.0 + 0.15 * jax.random.normal(arg_keys[3], (D,), jnp.float32), 0.25, 1.75),
        "weight_in": noise(arg_keys[4], (D, FFN_WIDTH), D ** -0.5, 0.1875, ((0, 64), (1, 4))),
        "weight_out": noise(arg_keys[5], (FFN_WIDTH, D), FFN_WIDTH ** -0.5, 0.09375, ((0, 256),)),
        "keep_count": draw_keep_count(jax.random.fold_in(arg_keys[8], 71), 0),
        "keep_index": draw_keep_index(jax.random.fold_in(arg_keys[8], 71), 0),
    }


norm_eps = 1e-05

def silu_grad(values):
    sigmoid = jax.nn.sigmoid(values)
    return sigmoid * (1.0 + values * (1.0 - sigmoid))

def reference(features, cotangent, conv_kernel, norm_gain, weight_in, weight_out, keep_count, keep_index):
    half_width = KERNEL // 2

    def utterance_step(totals, inputs):
        grad_in_sum, grad_out_sum, kernel_sum, gain_sum = totals
        frames, upstream, counts, indices = inputs
        frames32 = frames.astype(jnp.float32)
        padded = jnp.pad(frames32, ((half_width, half_width), (0, 0)))
        conv_out = jnp.zeros((FRAMES, D), jnp.float32)
        for offset in range(KERNEL):
            conv_out = conv_out + conv_kernel[offset] * padded[offset:offset + FRAMES]
        hidden = (frames32 + jax.nn.silu(conv_out)).astype(jnp.bfloat16)
        blocks = (counts + BLOCK - 1) // BLOCK
        starts = jnp.cumsum(blocks) - blocks
        block_ids = jnp.arange(SHARDS * KEPT, dtype=jnp.int32)
        owner_shard = lax.optimization_barrier(jnp.sum((starts[None, :] <= block_ids[:, None]).astype(jnp.int32), axis=1)) - 1
        slot_ids = jnp.arange(SHARDS * KEPT * BLOCK, dtype=jnp.int32)
        slot_owner = jnp.repeat(owner_shard, BLOCK)
        within = (slot_ids // BLOCK - starts[slot_owner]) * BLOCK + slot_ids % BLOCK
        valid_slot = within < counts[slot_owner]
        flat_index = (slot_owner * FRAMES_DEV + jnp.minimum(within, FRAMES_DEV - 1)).astype(jnp.int32)
        frame_at = (slot_owner * FRAMES_DEV + indices[flat_index]).astype(jnp.int32)
        zero_bf = jnp.zeros((), jnp.bfloat16)
        kept_hidden = jnp.where(valid_slot[:, None], hidden[frame_at], zero_bf)
        kept_grad = jnp.where(valid_slot[:, None], upstream[frame_at], zero_bf)
        rows32 = kept_hidden.astype(jnp.float32)
        row_mean = lax.optimization_barrier(jnp.mean(rows32, axis=1, keepdims=True))
        centred = rows32 - row_mean
        row_var = lax.optimization_barrier(jnp.mean(centred * centred, axis=1, keepdims=True))
        inv_scale = lax.rsqrt(row_var + norm_eps)
        normed = centred * inv_scale
        scaled = (normed * norm_gain).astype(jnp.bfloat16)
        pre_act = jnp.dot(scaled, weight_in, preferred_element_type=jnp.float32)
        activation = jax.nn.silu(pre_act).astype(jnp.bfloat16)
        grad_out_sum = grad_out_sum + 0.5 * jnp.dot(activation.T, kept_grad, preferred_element_type=jnp.float32)
        act_grad = 0.5 * jnp.dot(kept_grad, weight_out.T, preferred_element_type=jnp.float32)
        up_grad = (act_grad * silu_grad(pre_act)).astype(jnp.bfloat16)
        grad_in_sum = grad_in_sum + jnp.dot(scaled.T, up_grad, preferred_element_type=jnp.float32)
        norm_grad = jnp.dot(up_grad, weight_in.T, preferred_element_type=jnp.float32)
        gain_sum = gain_sum + lax.optimization_barrier(jnp.sum(norm_grad * normed, axis=0))
        gain_grad = norm_grad * norm_gain
        back_term = (gain_grad - lax.optimization_barrier(jnp.mean(gain_grad, axis=1, keepdims=True)) - normed * lax.optimization_barrier(jnp.mean(gain_grad * normed, axis=1, keepdims=True))) * inv_scale
        row_grad = (kept_grad.astype(jnp.float32) + back_term).astype(jnp.bfloat16)
        frame_grad = jnp.zeros((FRAMES, D), jnp.float32).at[frame_at].add(jnp.where(valid_slot[:, None], row_grad.astype(jnp.float32), 0.0))
        conv_grad = frame_grad * silu_grad(conv_out)
        grad_pad = jnp.pad(conv_grad, ((half_width, half_width), (0, 0)))
        transposed = jnp.zeros((FRAMES, D), jnp.float32)
        for offset in range(KERNEL):
            begin = 2 * half_width - offset
            transposed = transposed + conv_kernel[offset] * grad_pad[begin:begin + FRAMES]
        kernel_term = jnp.stack([lax.optimization_barrier(jnp.sum(conv_grad * padded[offset:offset + FRAMES], axis=0)) for offset in range(KERNEL)])
        kernel_sum = kernel_sum + kernel_term
        grad_x = (frame_grad + transposed).astype(jnp.bfloat16)
        return ((grad_in_sum, grad_out_sum, kernel_sum, gain_sum), grad_x)
    start_totals = (jnp.zeros((D, FFN_WIDTH), jnp.float32), jnp.zeros((FFN_WIDTH, D), jnp.float32), jnp.zeros((KERNEL, D), jnp.float32), jnp.zeros((D,), jnp.float32))
    totals, grad_features = lax.scan(utterance_step, start_totals, (features, cotangent, keep_count, keep_index))
    return (grad_features, totals[0], totals[1], totals[2], totals[3])
```

```python
import jax
import jax.numpy as jnp
from jax import lax
from jax.sharding import Mesh, PartitionSpec as P

norm_eps = 1e-05
BLOCK = 128
SEQ = ("y", "z", "core")
f32 = jnp.float32
bf16 = jnp.bfloat16


def shift(cells, axis, by):
    count = lax.axis_size(axis)
    return lax.ppermute(cells, axis, [(i, i + by) for i in range(count) if 0 <= i + by < count])


def turn(cells, axis, by):
    count = lax.axis_size(axis)
    return lax.ppermute(cells, axis, [(i, (i + by) % count) for i in range(count)])


def with_halo(cells, width):
    head = cells[:width]
    tail = cells[cells.shape[0] - width :]
    return jnp.concatenate([shift(tail, SEQ, 1), cells, shift(head, SEQ, -1)], axis=0)


def exchange(cells, axis):
    return lax.all_to_all(cells, axis, 0, 0, tiled=True)


def spread(cells, axis):
    count = lax.axis_size(axis)
    return exchange(jnp.broadcast_to(cells[None], (count,) + cells.shape), axis)


def ring_gather(cells, axis):
    count = lax.axis_size(axis)
    me = lax.axis_index(axis)
    out = jnp.zeros((count,) + cells.shape, cells.dtype)

    def put(out, piece, owner):
        return lax.dynamic_update_slice_in_dim(out, piece[None], owner % count, 0)

    out = put(out, cells, me)
    ahead = behind = cells
    for step in range(1, count // 2 + 1):
        ahead = turn(ahead, axis, 1)
        out = put(out, ahead, me - step + count)
        if 2 * step < count:
            behind = turn(behind, axis, -1)
            out = put(out, behind, me + step)
    return out


def silu_grad(values):
    sigmoid = jax.nn.sigmoid(values)
    return sigmoid * (1.0 + values * (1.0 - sigmoid))


def per_device(
    features, cotangent, conv_kernel, norm_gain, weight_in, weight_out, keep_count, keep_index
):
    frames = features[0]
    length, width = frames.shape
    tap_count = conv_kernel.shape[0]
    half_width = tap_count // 2
    shard = lax.axis_index(SEQ)
    core = lax.axis_index("core")
    ny, nz = lax.axis_size("y"), lax.axis_size("z")
    rows_in = weight_in.shape[0]
    hidden_dev = weight_in.shape[1]

    pair = jnp.stack([weight_in, weight_out])
    pieces = ring_gather(spread(pair, "y"), "z")
    others = turn(pieces, "core", 1)
    both = jnp.stack([jnp.where(core == 0, pieces, others), jnp.where(core == 0, others, pieces)])
    both = both.transpose(3, 2, 1, 0, 4, 5)
    w_in = both[0].reshape(width, hidden_dev)
    w_out = both[1].reshape(hidden_dev, width)

    counts = keep_count[0]
    blocks = (counts + BLOCK - 1) // BLOCK
    before = jnp.sum(jnp.where(jnp.arange(counts.shape[0]) < shard, blocks, 0))
    late = before - shard > 0
    local_index = keep_index[0]
    valid = jnp.arange(length, dtype=jnp.int32) < counts[shard]
    zero_bf = jnp.zeros((), bf16)

    def place(rows):
        going = jnp.where(late, rows[:BLOCK], rows[BLOCK:])
        came = shift(going, SEQ, 1)
        return jnp.where(late, came, rows[:BLOCK])

    picked_grad = place(jnp.where(valid[:, None], cotangent[0][local_index], zero_bf))
    grad_all = spread(picked_grad, "utt").reshape(-1, width)

    wide_rows = with_halo(frames, half_width)
    wide32 = wide_rows.astype(f32)
    conv_out = jnp.zeros((length, width), f32)
    for offset in range(tap_count):
        conv_out = conv_out + conv_kernel[offset] * wide32[offset : offset + length]
    hidden = (frames.astype(f32) + jax.nn.silu(conv_out)).astype(bf16)
    picked = place(jnp.where(valid[:, None], hidden[local_index], zero_bf))
    rows32 = picked.astype(f32)
    row_mean = jnp.mean(rows32, axis=1, keepdims=True)
    centred = rows32 - row_mean
    row_var = jnp.mean(centred * centred, axis=1, keepdims=True)
    inv_scale = lax.rsqrt(row_var + norm_eps)
    normed = centred * inv_scale
    scaled = (normed * norm_gain).astype(bf16)
    scaled_all = spread(scaled, "utt").reshape(-1, width)

    pre_act = jnp.dot(scaled_all, w_in, preferred_element_type=f32)
    activation = jax.nn.silu(pre_act).astype(bf16)
    act_grad = 0.5 * lax.dot_general(
        grad_all, w_out, (((1,), (1,)), ((), ())), preferred_element_type=f32
    )
    up_grad = (act_grad * silu_grad(pre_act)).astype(bf16)
    partial_grad = lax.dot_general(
        up_grad, w_in, (((1,), (1,)), ((), ())), preferred_element_type=f32
    )
    parts = exchange(partial_grad.astype(bf16).reshape(-1, BLOCK, width), "utt")
    norm_grad = jnp.sum(parts.astype(f32), axis=0)

    over_rows = (((0,), (0,)), ((), ()))
    g_in = lax.dot_general(scaled_all, up_grad, over_rows, preferred_element_type=f32)
    g_out = 0.5 * lax.dot_general(activation, grad_all, over_rows, preferred_element_type=f32)
    grads = jnp.stack(
        [
            g_in.reshape(ny, nz, 2, rows_in, hidden_dev),
            g_out.reshape(ny, nz, 2, rows_in, width),
        ],
        axis=2,
    )
    first, second = grads[:, :, :, 0], grads[:, :, :, 1]
    theirs = jnp.where(core == 0, second, first).astype(bf16)
    mine = jnp.where(core == 0, first, second)
    chip = (mine + turn(theirs, "core", 1).astype(f32)).astype(bf16)
    chip = jnp.sum(exchange(chip, "y").astype(f32), axis=0).astype(bf16)
    chip = jnp.sum(exchange(chip, "z").astype(f32), axis=0)
    grad_weight_in, grad_weight_out = chip[0], chip[1]

    gain_term = jnp.sum(norm_grad * normed, axis=0)
    gain_grad = norm_grad * norm_gain
    back_term = (
        gain_grad
        - jnp.mean(gain_grad, axis=1, keepdims=True)
        - normed * jnp.mean(gain_grad * normed, axis=1, keepdims=True)
    ) * inv_scale
    row_grad = (picked_grad.astype(f32) + back_term).astype(bf16)
    returned = shift(row_grad, SEQ, -1)
    low = jnp.where(late, returned, row_grad)
    high = returned
    local_grad = jnp.concatenate([low, high]).astype(f32)
    frame_grad = (
        jnp.zeros((length, width), f32)
        .at[local_index]
        .add(jnp.where(valid[:, None], local_grad, 0.0))
    )
    conv_grad = frame_grad * silu_grad(conv_out)
    grad_wide = with_halo(conv_grad, half_width)
    kernel_term = [
        jnp.sum(conv_grad * wide32[offset : offset + length], axis=0)
        for offset in range(tap_count)
    ]
    transposed = jnp.zeros((length, width), f32)
    for offset in range(tap_count):
        begin = 2 * half_width - offset
        transposed = transposed + conv_kernel[offset] * grad_wide[begin : begin + length]
    grad_x = (frame_grad + transposed).astype(bf16)

    small = jnp.stack(kernel_term + [gain_term])
    half = small.shape[0] // 2
    own = jnp.where(core == 0, small[:half], small[half:])
    gone = jnp.where(core == 0, small[half:], small[:half])
    total = own + turn(gone, "core", 1)
    for axis in ("utt", "y", "z"):
        total = jnp.sum(spread(total, axis), axis=0)
    back = turn(total, "core", 1)
    full = jnp.concatenate([jnp.where(core == 0, total, back), jnp.where(core == 0, back, total)])
    return (grad_x[None], grad_weight_in, grad_weight_out, full[:tap_count], full[tap_count])


def solution(mesh):
    utts = mesh.shape["utt"]
    fine = Mesh(mesh.devices.reshape(4, 8, 2, utts), ("y", "z", "core", "utt"))
    placed = (
        P("utt", SEQ, None),
        P("utt", SEQ, None),
        P(),
        P(),
        P(SEQ, "utt"),
        P(("utt",) + SEQ, None),
        P("utt", None),
        P("utt", SEQ),
    )
    return jax.shard_map(
        per_device,
        mesh=fine,
        in_specs=placed,
        out_specs=(P("utt", SEQ, None), P(SEQ, "utt"), P(("utt",) + SEQ, None), P(), P()),
        check_vma=False,
    )
```

```python
import jax
import jax.numpy as jnp
from jax import lax
from jax.experimental.layout import Layout, with_layout_constraint
from jax.sharding import Mesh, PartitionSpec as P

norm_eps = 1e-05
BLOCK = 128
SEQ = ("y", "z", "core")
f32 = jnp.float32
bf16 = jnp.bfloat16


def shift(cells, axis, by):
    count = lax.axis_size(axis)
    return lax.ppermute(cells, axis, [(i, i + by) for i in range(count) if 0 <= i + by < count])


def turn(cells, axis, by):
    count = lax.axis_size(axis)
    return lax.ppermute(cells, axis, [(i, (i + by) % count) for i in range(count)])


def with_halo(cells, width):
    head = cells[:width]
    tail = cells[cells.shape[0] - width :]
    return jnp.concatenate([shift(tail, SEQ, 1), cells, shift(head, SEQ, -1)], axis=0)


def exchange(cells, axis):
    return lax.all_to_all(cells, axis, 0, 0, tiled=True)


def spread(cells, axis):
    count = lax.axis_size(axis)
    return exchange(jnp.broadcast_to(cells[None], (count,) + cells.shape), axis)


def pick(cells, which, axis):
    return lax.dynamic_index_in_dim(cells, which, axis, keepdims=False)


def gather_weights(pair, core):
    half = spread(pair, "z")
    half = spread(half, "y")
    other = turn(half, "core", 1)
    first = jnp.where(core == 0, half, other)
    second = jnp.where(core == 0, other, half)
    both = jnp.stack([first, second], axis=3)
    width = pair.shape[-1]
    return [both[:, :, i].reshape(-1, width) for i in range(2)]


def scatter_grads(grads, core, rows):
    ny, nz = lax.axis_size("y"), lax.axis_size("z")
    cells = [g.reshape(ny, nz, 2, rows, g.shape[1]) for g in grads]
    theirs = jnp.concatenate([pick(c, 1 - core, 2).astype(bf16) for c in cells], axis=1)
    came = turn(theirs, "core", 1)
    mine = jnp.concatenate([pick(c, core, 2) for c in cells], axis=1)
    chip = (mine + came.astype(f32)).astype(bf16)
    spot = lax.axis_index("y")
    leave = [pick(chip, (spot + by) % ny, 0) for by in range(ny)]
    came = [turn(leave[by], "y", by) for by in range(1, ny)]
    chip = leave[0].astype(f32)
    for part in came:
        chip = chip + part.astype(f32)
    chip = chip.astype(bf16)
    chip = chip.reshape((2, nz) + chip.shape[1:]).transpose(1, 0, 2, 3)
    chip = exchange(chip, "z")
    return jnp.sum(chip.astype(f32), axis=0)


def silu_grad(values):
    sigmoid = jax.nn.sigmoid(values)
    return sigmoid * (1.0 + values * (1.0 - sigmoid))


def per_device(
    features, cotangent, conv_kernel, norm_gain, weight_in, weight_out, keep_count, keep_index
):
    frames = features[0]
    length, width = frames.shape
    tap_count = conv_kernel.shape[0]
    half_width = tap_count // 2
    shard = lax.axis_index(SEQ)
    core = lax.axis_index("core")
    rows_in = weight_in.shape[0]

    w_in, w_out = gather_weights(jnp.stack([weight_in, weight_out]), core)

    counts = keep_count[0]
    blocks = (counts + BLOCK - 1) // BLOCK
    before = jnp.sum(jnp.where(jnp.arange(counts.shape[0]) < shard, blocks, 0))
    late = before - shard > 0
    local_index = keep_index[0]
    valid = jnp.arange(length, dtype=jnp.int32) < counts[shard]
    zero_bf = jnp.zeros((), bf16)

    def place(rows):
        going = jnp.where(late, rows[:, :BLOCK], rows[:, BLOCK:])
        came = shift(going, SEQ, 1)
        return jnp.where(late, came, rows[:, :BLOCK])

    wide_rows = with_halo(frames, half_width)
    wide32 = wide_rows.astype(f32)
    conv_out = jnp.zeros((length, width), f32)
    for offset in range(tap_count):
        conv_out = conv_out + conv_kernel[offset] * wide32[offset : offset + length]
    hidden = (frames.astype(f32) + jax.nn.silu(conv_out)).astype(bf16)
    kept = jnp.stack([hidden[local_index], cotangent[0][local_index]])
    picked, picked_grad = place(jnp.where(valid[:, None], kept, zero_bf))
    rows32 = picked.astype(f32)
    row_mean = jnp.mean(rows32, axis=1, keepdims=True)
    centred = rows32 - row_mean
    row_var = jnp.mean(centred * centred, axis=1, keepdims=True)
    inv_scale = lax.rsqrt(row_var + norm_eps)
    normed = centred * inv_scale
    scaled = (normed * norm_gain).astype(bf16)
    payload = jnp.stack([scaled, picked_grad])
    utts = lax.axis_size("utt")
    arrived = [payload] + [turn(payload, "utt", by) for by in range(1, utts)]
    scaled_all, grad_all = (jnp.concatenate([a[i] for a in arrived]) for i in range(2))
    plain = Layout(major_to_minor=(0, 1))
    grad_all = with_layout_constraint(grad_all, plain)

    pre_act = jnp.dot(scaled_all, w_in, preferred_element_type=f32)
    activation = jax.nn.silu(pre_act).astype(bf16)
    act_grad = 0.5 * lax.dot_general(
        grad_all, w_out, (((1,), (1,)), ((), ())), preferred_element_type=f32
    )
    up_grad = (act_grad * silu_grad(pre_act)).astype(bf16)
    partial_grad = lax.dot_general(
        up_grad, w_in, (((1,), (1,)), ((), ())), preferred_element_type=f32
    )
    parts = partial_grad.reshape(utts, BLOCK, width)
    norm_grad = parts[0]
    owed = [turn(parts[by].astype(bf16), "utt", -by) for by in range(1, utts)]
    for part in owed:
        norm_grad = norm_grad + part.astype(f32)

    over_rows = (((0,), (0,)), ((), ()))
    g_out = 0.5 * lax.dot_general(activation, grad_all, over_rows, preferred_element_type=f32)
    g_in = lax.dot_general(scaled_all, up_grad, over_rows, preferred_element_type=f32)
    grad_weight_in, grad_weight_out = scatter_grads([g_in, g_out], core, rows_in)

    gain_term = jnp.sum(norm_grad * normed, axis=0)
    gain_grad = norm_grad * norm_gain
    back_term = (
        gain_grad
        - jnp.mean(gain_grad, axis=1, keepdims=True)
        - normed * jnp.mean(gain_grad * normed, axis=1, keepdims=True)
    ) * inv_scale
    row_grad = (picked_grad.astype(f32) + back_term).astype(bf16)
    returned = shift(row_grad, SEQ, -1)
    low = jnp.where(late, returned, row_grad)
    high = returned
    local_grad = jnp.concatenate([low, high]).astype(f32)
    frame_grad = (
        jnp.zeros((length, width), f32)
        .at[local_index]
        .add(jnp.where(valid[:, None], local_grad, 0.0))
    )
    conv_grad = frame_grad * silu_grad(conv_out)
    grad_wide = with_halo(conv_grad, half_width)
    kernel_term = [
        jnp.sum(conv_grad * wide32[offset : offset + length], axis=0)
        for offset in range(tap_count)
    ]
    transposed = jnp.zeros((length, width), f32)
    for offset in range(tap_count):
        begin = 2 * half_width - offset
        transposed = transposed + conv_kernel[offset] * grad_wide[begin : begin + length]
    grad_x = (frame_grad + transposed).astype(bf16)

    small = jnp.stack(kernel_term + [gain_term])
    near = ("core", "utt")
    part = exchange(small.reshape(lax.axis_size(near), 8, -1), near)
    part = jnp.sum(part, axis=0)
    part = spread(part, ("y", "z"))
    part = jnp.sum(part, axis=0)
    full = spread(part, near)
    full = full.reshape(small.shape)
    return (grad_x[None], grad_weight_in, grad_weight_out, full[:tap_count], full[tap_count])


def solution(mesh):
    utts = mesh.shape["utt"]
    fine = Mesh(mesh.devices.reshape(4, 8, 2, utts), ("y", "z", "core", "utt"))
    placed = (
        P("utt", SEQ, None),
        P("utt", SEQ, None),
        P(),
        P(),
        P(SEQ, "utt"),
        P(("utt",) + SEQ, None),
        P("utt", None),
        P("utt", SEQ),
    )
    return jax.shard_map(
        per_device,
        mesh=fine,
        in_specs=placed,
        out_specs=(P("utt", SEQ, None), P(SEQ, "utt"), P(("utt",) + SEQ, None), P(), P()),
        check_vma=False,
    )
```

```python
import jax
import jax.numpy as jnp
from jax import lax
from jax.experimental.layout import Layout, with_layout_constraint
from jax.sharding import Mesh, PartitionSpec as P

norm_eps = 1e-05
BLOCK = 128
SEQ = ("y", "z", "core")
f32 = jnp.float32
bf16 = jnp.bfloat16


def shift(cells, axis, by):
    count = lax.axis_size(axis)
    return lax.ppermute(cells, axis, [(i, i + by) for i in range(count) if 0 <= i + by < count])


def turn(cells, axis, by):
    count = lax.axis_size(axis)
    return lax.ppermute(cells, axis, [(i, (i + by) % count) for i in range(count)])


def with_halo(cells, width):
    head = cells[:width]
    tail = cells[cells.shape[0] - width :]
    return jnp.concatenate([shift(tail, SEQ, 1), cells, shift(head, SEQ, -1)], axis=0)


def exchange(cells, axis):
    return lax.all_to_all(cells, axis, 0, 0, tiled=True)


def spread(cells, axis):
    count = lax.axis_size(axis)
    return exchange(jnp.broadcast_to(cells[None], (count,) + cells.shape), axis)


def pick(cells, which, axis):
    return lax.dynamic_index_in_dim(cells, which, axis, keepdims=False)


def gather_weights(pair, core):
    half = spread(pair, "z")
    half = spread(half, "y")
    other = turn(half, "core", 1)
    first = jnp.where(core == 0, half, other)
    second = jnp.where(core == 0, other, half)
    both = jnp.stack([first, second], axis=3)
    width = pair.shape[-1]
    return [both[:, :, i].reshape(-1, width) for i in range(2)]


def scatter_grads(grads, core, rows):
    ny, nz = lax.axis_size("y"), lax.axis_size("z")
    cells = [g.reshape(ny, nz, 2, rows, g.shape[1]) for g in grads]
    theirs = jnp.concatenate([pick(c, 1 - core, 2) for c in cells], axis=1)
    mine = jnp.concatenate([pick(c, core, 2) for c in cells], axis=1)
    came = turn(theirs, "core", 1)
    chip = (mine.astype(f32) + came.astype(f32)).astype(bf16)
    spot = lax.axis_index("y")
    leave = [pick(chip, (spot + by) % ny, 0) for by in range(ny)]
    came = [turn(leave[by], "y", by) for by in range(1, ny)]
    chip = leave[0].astype(f32)
    for part in came:
        chip = chip + part.astype(f32)
    return chip.astype(bf16).reshape((2, nz) + chip.shape[1:]).transpose(1, 0, 2, 3)


def silu_grad(values):
    sigmoid = jax.nn.sigmoid(values)
    return sigmoid * (1.0 + values * (1.0 - sigmoid))


def per_device(
    features, cotangent, conv_kernel, norm_gain, weight_in, weight_out, keep_count, keep_index
):
    frames = features[0]
    length, width = frames.shape
    tap_count = conv_kernel.shape[0]
    half_width = tap_count // 2
    shard = lax.axis_index(SEQ)
    core = lax.axis_index("core")
    rows_in = weight_in.shape[0]

    w_in, w_out = gather_weights(jnp.stack([weight_in, weight_out]), core)

    counts = keep_count[0]
    blocks = (counts + BLOCK - 1) // BLOCK
    before = jnp.sum(jnp.where(jnp.arange(counts.shape[0]) < shard, blocks, 0))
    late = before - shard > 0
    local_index = keep_index[0]
    valid = jnp.arange(length, dtype=jnp.int32) < counts[shard]
    zero_bf = jnp.zeros((), bf16)

    def place(rows):
        going = jnp.where(late, rows[:, :BLOCK], rows[:, BLOCK:])
        came = shift(going, SEQ, 1)
        return jnp.where(late, came, rows[:, :BLOCK])

    wide_rows = with_halo(frames, half_width)
    wide32 = wide_rows.astype(f32)
    conv_out = jnp.zeros((length, width), f32)
    for offset in range(tap_count):
        conv_out = conv_out + conv_kernel[offset] * wide32[offset : offset + length]
    hidden = (frames.astype(f32) + jax.nn.silu(conv_out)).astype(bf16)
    kept = jnp.stack([hidden[local_index], cotangent[0][local_index]])
    picked, picked_grad = place(jnp.where(valid[:, None], kept, zero_bf))
    rows32 = picked.astype(f32)
    row_mean = jnp.mean(rows32, axis=1, keepdims=True)
    centred = rows32 - row_mean
    row_var = jnp.mean(centred * centred, axis=1, keepdims=True)
    inv_scale = lax.rsqrt(row_var + norm_eps)
    normed = centred * inv_scale
    scaled = (normed * norm_gain).astype(bf16)
    payload = jnp.stack([scaled, picked_grad])
    utts = lax.axis_size("utt")
    arrived = [payload] + [turn(payload, "utt", by) for by in range(1, utts)]
    scaled_all, grad_all = (jnp.concatenate([a[i] for a in arrived]) for i in range(2))
    plain = Layout(major_to_minor=(0, 1))
    grad_all = with_layout_constraint(grad_all, plain)

    pre_act = jnp.dot(scaled_all, w_in, preferred_element_type=f32)
    activation = jax.nn.silu(pre_act).astype(bf16)
    act_grad = 0.5 * lax.dot_general(
        grad_all, w_out, (((1,), (1,)), ((), ())), preferred_element_type=f32
    )
    up_grad = (act_grad * silu_grad(pre_act)).astype(bf16)
    partial_grad = lax.dot_general(
        up_grad, w_in, (((1,), (1,)), ((), ())), preferred_element_type=f32
    )
    parts = partial_grad.reshape(utts, BLOCK, width)
    norm_grad = parts[0]
    owed = [turn(parts[by].astype(bf16), "utt", -by) for by in range(1, utts)]
    for part in owed:
        norm_grad = norm_grad + part.astype(f32)

    over_rows = (((0,), (0,)), ((), ()))
    g_out = 0.5 * lax.dot_general(activation, grad_all, over_rows, preferred_element_type=f32)
    g_in = lax.dot_general(scaled_all, up_grad, over_rows, preferred_element_type=f32)
    g_out, g_in = g_out.astype(bf16), g_in.astype(bf16)
    chip = scatter_grads([g_in, g_out], core, rows_in)

    gain_term = jnp.sum(norm_grad * normed, axis=0)
    gain_grad = norm_grad * norm_gain
    back_term = (
        gain_grad
        - jnp.mean(gain_grad, axis=1, keepdims=True)
        - normed * jnp.mean(gain_grad * normed, axis=1, keepdims=True)
    ) * inv_scale
    row_grad = (picked_grad.astype(f32) + back_term).astype(bf16)
    returned = shift(row_grad, SEQ, -1)
    low = jnp.where(late, returned, row_grad)
    high = returned
    local_grad = jnp.concatenate([low, high]).astype(f32)
    frame_grad = (
        jnp.zeros((length, width), f32)
        .at[local_index]
        .add(jnp.where(valid[:, None], local_grad, 0.0))
    )
    conv_grad = frame_grad * silu_grad(conv_out)
    grad_wide = with_halo(conv_grad, half_width)
    kernel_term = [
        jnp.sum(conv_grad * wide32[offset : offset + length], axis=0)
        for offset in range(tap_count)
    ]
    transposed = jnp.zeros((length, width), f32)
    for offset in range(tap_count):
        begin = 2 * half_width - offset
        transposed = transposed + conv_kernel[offset] * grad_wide[begin : begin + length]
    grad_x = (frame_grad + transposed).astype(bf16)[None]

    small = jnp.stack(kernel_term + [gain_term])
    nz = lax.axis_size("z")
    rounded = lax.reduce_precision(small, 8, 7)
    value = rounded.astype(bf16)
    rest = (small - rounded).astype(bf16)
    lanes = small.reshape(nz, -1, width).shape[1]
    load = jnp.concatenate(
        [chip.reshape(nz, -1, width), value.reshape(nz, -1, width), rest.reshape(nz, -1, width)],
        axis=1,
    )
    load = exchange(load, "z")
    load = jnp.sum(load.astype(f32), axis=0)
    grad_weight_in, grad_weight_out = load[:rows_in], load[rows_in : 2 * rows_in]
    part = load[2 * rows_in : 2 * rows_in + lanes] + load[2 * rows_in + lanes :]
    part = spread(part.reshape(8, -1), ("y", "core", "utt"))
    part = jnp.sum(part, axis=0)
    full = spread(part, "z")
    full = full.reshape(small.shape)
    return (grad_x, grad_weight_in, grad_weight_out, full[:tap_count], full[tap_count])


def solution(mesh):
    utts = mesh.shape["utt"]
    fine = Mesh(mesh.devices.reshape(4, 8, 2, utts), ("y", "z", "core", "utt"))
    placed = (
        P("utt", SEQ, None),
        P("utt", SEQ, None),
        P(),
        P(),
        P(SEQ, "utt"),
        P(("utt",) + SEQ, None),
        P("utt", None),
        P("utt", SEQ),
    )
    return jax.shard_map(
        per_device,
        mesh=fine,
        in_specs=placed,
        out_specs=(P("utt", SEQ, None), P(SEQ, "utt"), P(("utt",) + SEQ, None), P(), P()),
        check_vma=False,
    )
```

```python
import jax
import jax.numpy as jnp
from jax import lax
from jax.experimental.layout import Layout, with_layout_constraint
from jax.sharding import Mesh, PartitionSpec as P

norm_eps = 1e-05
BLOCK = 128
SEQ = ("y", "z", "core")
f32 = jnp.float32
bf16 = jnp.bfloat16


def shift(cells, axis, by):
    count = lax.axis_size(axis)
    return lax.ppermute(cells, axis, [(i, i + by) for i in range(count) if 0 <= i + by < count])


def turn(cells, axis, by):
    count = lax.axis_size(axis)
    return lax.ppermute(cells, axis, [(i, (i + by) % count) for i in range(count)])


def with_halo(cells, width):
    head = cells[:width]
    tail = cells[cells.shape[0] - width :]
    return jnp.concatenate([shift(tail, SEQ, 1), cells, shift(head, SEQ, -1)], axis=0)


def exchange(cells, axis):
    return lax.all_to_all(cells, axis, 0, 0, tiled=True)


def spread(cells, axis):
    count = lax.axis_size(axis)
    return exchange(jnp.broadcast_to(cells[None], (count,) + cells.shape), axis)


def pick(cells, which, axis):
    return lax.dynamic_index_in_dim(cells, which, axis, keepdims=False)


def gather_weights(pair, core):
    half = spread(pair, "z")
    half = spread(half, "y")
    half = with_layout_constraint(half, Layout(major_to_minor=(0, 1, 2, 3, 4)))
    other = turn(half, "core", 1)
    width = pair.shape[-1]
    whole = []
    for i in range(2):
        ours, came = half[:, :, i], other[:, :, i]
        both = [jnp.where(core == 0, ours, came), jnp.where(core == 0, came, ours)]
        whole.append(jnp.stack(both, axis=2).reshape(-1, width))
    return whole


def scatter_grads(grads, core, rows):
    ny, nz = lax.axis_size("y"), lax.axis_size("z")
    cells = [g.reshape(ny, nz, 2, rows, g.shape[1]) for g in grads]
    theirs = jnp.concatenate([pick(c, 1 - core, 2) for c in cells], axis=1)
    mine = jnp.concatenate([pick(c, core, 2) for c in cells], axis=1)
    came = turn(theirs, "core", 1)
    chip = (mine.astype(f32) + came.astype(f32)).astype(bf16)
    spot = lax.axis_index("y")
    leave = [pick(chip, (spot + by) % ny, 0) for by in range(ny)]
    came = [turn(leave[by], "y", by) for by in range(1, ny)]
    chip = leave[0].astype(f32)
    for part in came:
        chip = chip + part.astype(f32)
    return chip.astype(bf16).reshape((2, nz) + chip.shape[1:]).transpose(1, 0, 2, 3)


def silu_grad(values):
    sigmoid = jax.nn.sigmoid(values)
    return sigmoid * (1.0 + values * (1.0 - sigmoid))


def per_device(
    features, cotangent, conv_kernel, norm_gain, weight_in, weight_out, keep_count, keep_index
):
    frames = features[0]
    length, width = frames.shape
    tap_count = conv_kernel.shape[0]
    half_width = tap_count // 2
    shard = lax.axis_index(SEQ)
    core = lax.axis_index("core")
    rows_in = weight_in.shape[0]

    w_in, w_out = gather_weights(jnp.stack([weight_in, weight_out]), core)

    counts = keep_count[0]
    blocks = (counts + BLOCK - 1) // BLOCK
    before = jnp.sum(jnp.where(jnp.arange(counts.shape[0]) < shard, blocks, 0))
    late = before - shard > 0
    local_index = keep_index[0]
    valid = jnp.arange(length, dtype=jnp.int32) < counts[shard]
    zero_bf = jnp.zeros((), bf16)

    def place(rows):
        going = jnp.where(late, rows[:, :BLOCK], rows[:, BLOCK:])
        came = shift(going, SEQ, 1)
        return jnp.where(late, came, rows[:, :BLOCK])

    wide_rows = with_halo(frames, half_width)
    wide32 = wide_rows.astype(f32)
    conv_out = jnp.zeros((length, width), f32)
    for offset in range(tap_count):
        conv_out = conv_out + conv_kernel[offset] * wide32[offset : offset + length]
    hidden = (frames.astype(f32) + jax.nn.silu(conv_out)).astype(bf16)
    kept = jnp.stack([hidden[local_index], cotangent[0][local_index]])
    picked, picked_grad = place(jnp.where(valid[:, None], kept, zero_bf))
    rows32 = picked.astype(f32)
    row_mean = jnp.mean(rows32, axis=1, keepdims=True)
    centred = rows32 - row_mean
    row_var = jnp.mean(centred * centred, axis=1, keepdims=True)
    inv_scale = lax.rsqrt(row_var + norm_eps)
    normed = centred * inv_scale
    scaled = (normed * norm_gain).astype(bf16)
    payload = jnp.stack([scaled, picked_grad])
    utts = lax.axis_size("utt")
    arrived = [payload] + [turn(payload, "utt", by) for by in range(1, utts)]
    scaled_all, grad_all = (jnp.concatenate([a[i] for a in arrived]) for i in range(2))
    plain = Layout(major_to_minor=(0, 1))
    grad_all = with_layout_constraint(grad_all, plain)

    pre_act = jnp.dot(scaled_all, w_in, preferred_element_type=f32)
    activation = jax.nn.silu(pre_act).astype(bf16)
    act_grad = 0.5 * lax.dot_general(
        grad_all, w_out, (((1,), (1,)), ((), ())), preferred_element_type=f32
    )
    up_grad = (act_grad * silu_grad(pre_act)).astype(bf16)
    partial_grad = lax.dot_general(
        up_grad, w_in, (((1,), (1,)), ((), ())), preferred_element_type=f32
    )
    parts = partial_grad.reshape(utts, BLOCK, width)
    norm_grad = parts[0]
    owed = [turn(parts[by].astype(bf16), "utt", -by) for by in range(1, utts)]
    for part in owed:
        norm_grad = norm_grad + part.astype(f32)

    over_rows = (((0,), (0,)), ((), ()))
    g_out = 0.5 * lax.dot_general(activation, grad_all, over_rows, preferred_element_type=f32)
    g_in = lax.dot_general(scaled_all, up_grad, over_rows, preferred_element_type=f32)
    g_out, g_in = g_out.astype(bf16), g_in.astype(bf16)
    chip = scatter_grads([g_in, g_out], core, rows_in)

    gain_term = jnp.sum(norm_grad * normed, axis=0)
    gain_grad = norm_grad * norm_gain
    back_term = (
        gain_grad
        - jnp.mean(gain_grad, axis=1, keepdims=True)
        - normed * jnp.mean(gain_grad * normed, axis=1, keepdims=True)
    ) * inv_scale
    row_grad = (picked_grad.astype(f32) + back_term).astype(bf16)
    returned = shift(row_grad, SEQ, -1)
    low = jnp.where(late, returned, row_grad)
    high = returned
    local_grad = jnp.concatenate([low, high]).astype(f32)
    frame_grad = (
        jnp.zeros((length, width), f32)
        .at[local_index]
        .add(jnp.where(valid[:, None], local_grad, 0.0))
    )
    conv_grad = frame_grad * silu_grad(conv_out)
    grad_wide = with_halo(conv_grad, half_width)
    kernel_term = [
        jnp.sum(conv_grad * wide32[offset : offset + length], axis=0)
        for offset in range(tap_count)
    ]
    transposed = jnp.zeros((length, width), f32)
    for offset in range(tap_count):
        begin = 2 * half_width - offset
        transposed = transposed + conv_kernel[offset] * grad_wide[begin : begin + length]
    grad_x = (frame_grad + transposed).astype(bf16)[None]

    small = jnp.stack(kernel_term + [gain_term])
    near = ("core", "utt")
    part = exchange(small.reshape(lax.axis_size(near), 8, -1), near)
    part = jnp.sum(part, axis=0)
    part = spread(part, ("y", "z"))
    part = jnp.sum(part, axis=0)
    full = spread(part, near)
    full = full.reshape(small.shape)
    load = exchange(chip, "z")
    grad_weight_in, grad_weight_out = jnp.sum(load.astype(f32), axis=0)
    return (grad_x, grad_weight_in, grad_weight_out, full[:tap_count], full[tap_count])


def solution(mesh):
    utts = mesh.shape["utt"]
    fine = Mesh(mesh.devices.reshape(4, 8, 2, utts), ("y", "z", "core", "utt"))
    placed = (
        P("utt", SEQ, None),
        P("utt", SEQ, None),
        P(),
        P(),
        P(SEQ, "utt"),
        P(("utt",) + SEQ, None),
        P("utt", None),
        P("utt", SEQ),
    )
    return jax.shard_map(
        per_device,
        mesh=fine,
        in_specs=placed,
        out_specs=(P("utt", SEQ, None), P(SEQ, "utt"), P(("utt",) + SEQ, None), P(), P()),
        check_vma=False,
    )
```

```python
import jax
import jax.numpy as jnp
from jax import lax
from jax.experimental.layout import Layout, with_layout_constraint
from jax.sharding import Mesh, PartitionSpec as P

norm_eps = 1e-05
BLOCK = 128
SEQ = ("y", "z", "core")
f32 = jnp.float32
bf16 = jnp.bfloat16


def shift(cells, axis, by):
    count = lax.axis_size(axis)
    return lax.ppermute(cells, axis, [(i, i + by) for i in range(count) if 0 <= i + by < count])


def turn(cells, axis, by):
    count = lax.axis_size(axis)
    return lax.ppermute(cells, axis, [(i, (i + by) % count) for i in range(count)])


def with_halo(cells, width):
    head = cells[:width]
    tail = cells[cells.shape[0] - width :]
    return jnp.concatenate([shift(tail, SEQ, 1), cells, shift(head, SEQ, -1)], axis=0)


def exchange(cells, axis):
    return lax.all_to_all(cells, axis, 0, 0, tiled=True)


def spread(cells, axis):
    count = lax.axis_size(axis)
    return exchange(jnp.broadcast_to(cells[None], (count,) + cells.shape), axis)


def pick(cells, which, axis):
    return lax.dynamic_index_in_dim(cells, which, axis, keepdims=False)


def gather_weights(pair, core):
    half = spread(pair, "z")
    half = spread(half, "y")
    half = with_layout_constraint(half, Layout(major_to_minor=(0, 1, 2, 3, 4)))
    other = turn(half, "core", 1)
    width = pair.shape[-1]
    whole = []
    for i in range(2):
        ours, came = half[:, :, i], other[:, :, i]
        both = [jnp.where(core == 0, ours, came), jnp.where(core == 0, came, ours)]
        whole.append(jnp.stack(both, axis=2).reshape(-1, width))
    return whole


def scatter_grads(grads, core, rows):
    ny, nz = lax.axis_size("y"), lax.axis_size("z")
    cells = [g.reshape(ny, nz, 2, rows, g.shape[1]) for g in grads]
    theirs = jnp.concatenate([pick(c, 1 - core, 2) for c in cells], axis=1)
    mine = jnp.concatenate([pick(c, core, 2) for c in cells], axis=1)
    came = turn(theirs, "core", 1)
    chip = (mine.astype(f32) + came.astype(f32)).astype(bf16)
    spot = lax.axis_index("y")
    leave = [pick(chip, (spot + by) % ny, 0) for by in range(ny)]
    came = [turn(leave[by], "y", by) for by in range(1, ny)]
    chip = leave[0].astype(f32)
    for part in came:
        chip = chip + part.astype(f32)
    return chip.astype(bf16).reshape((2, nz) + chip.shape[1:]).transpose(1, 0, 2, 3)


def silu_grad(values):
    sigmoid = jax.nn.sigmoid(values)
    return sigmoid * (1.0 + values * (1.0 - sigmoid))


def per_device(
    features, cotangent, conv_kernel, norm_gain, weight_in, weight_out, keep_count, keep_index
):
    frames = features[0]
    length, width = frames.shape
    tap_count = conv_kernel.shape[0]
    half_width = tap_count // 2
    shard = lax.axis_index(SEQ)
    core = lax.axis_index("core")
    rows_in = weight_in.shape[0]

    w_in, w_out = gather_weights(jnp.stack([weight_in, weight_out]), core)

    counts = keep_count[0]
    blocks = (counts + BLOCK - 1) // BLOCK
    before = jnp.sum(jnp.where(jnp.arange(counts.shape[0]) < shard, blocks, 0))
    late = before - shard > 0
    local_index = keep_index[0]
    valid = jnp.arange(length, dtype=jnp.int32) < counts[shard]
    zero_bf = jnp.zeros((), bf16)

    def place(rows):
        going = jnp.where(late, rows[:, :BLOCK], rows[:, BLOCK:])
        came = shift(going, SEQ, 1)
        return jnp.where(late, came, rows[:, :BLOCK])

    wide_rows = with_halo(frames, half_width)
    wide32 = wide_rows.astype(f32)
    conv_out = jnp.zeros((length, width), f32)
    for offset in range(tap_count):
        conv_out = conv_out + conv_kernel[offset] * wide32[offset : offset + length]
    hidden = (frames.astype(f32) + jax.nn.silu(conv_out)).astype(bf16)
    kept = jnp.stack([hidden[local_index], cotangent[0][local_index]])
    picked, picked_grad = place(jnp.where(valid[:, None], kept, zero_bf))
    rows32 = picked.astype(f32)
    row_mean = jnp.mean(rows32, axis=1, keepdims=True)
    centred = rows32 - row_mean
    row_var = jnp.mean(centred * centred, axis=1, keepdims=True)
    inv_scale = lax.rsqrt(row_var + norm_eps)
    normed = centred * inv_scale
    scaled = (normed * norm_gain).astype(bf16)
    payload = jnp.stack([scaled, picked_grad])
    utts = lax.axis_size("utt")
    arrived = [payload] + [turn(payload, "utt", by) for by in range(1, utts)]
    scaled_all, grad_all = (jnp.concatenate([a[i] for a in arrived]) for i in range(2))
    plain = Layout(major_to_minor=(0, 1))
    grad_all = with_layout_constraint(grad_all, plain)

    pre_act = jnp.dot(scaled_all, w_in, preferred_element_type=f32)
    activation = jax.nn.silu(pre_act).astype(bf16)
    act_grad = 0.5 * lax.dot_general(
        grad_all, w_out, (((1,), (1,)), ((), ())), preferred_element_type=f32
    )
    up_grad = (act_grad * silu_grad(pre_act)).astype(bf16)
    partial_grad = lax.dot_general(
        up_grad, w_in, (((1,), (1,)), ((), ())), preferred_element_type=f32
    )
    parts = partial_grad.reshape(utts, BLOCK, width)
    norm_grad = parts[0]
    owed = [turn(parts[by].astype(bf16), "utt", -by) for by in range(1, utts)]
    for part in owed:
        norm_grad = norm_grad + part.astype(f32)

    over_rows = (((0,), (0,)), ((), ()))
    g_out = 0.5 * lax.dot_general(activation, grad_all, over_rows, preferred_element_type=f32)
    g_in = lax.dot_general(scaled_all, up_grad, over_rows, preferred_element_type=f32)
    g_out, g_in = g_out.astype(bf16), g_in.astype(bf16)
    chip = scatter_grads([g_in, g_out], core, rows_in)

    gain_term = jnp.sum(norm_grad * normed, axis=0)
    gain_grad = norm_grad * norm_gain
    back_term = (
        gain_grad
        - jnp.mean(gain_grad, axis=1, keepdims=True)
        - normed * jnp.mean(gain_grad * normed, axis=1, keepdims=True)
    ) * inv_scale
    row_grad = (picked_grad.astype(f32) + back_term).astype(bf16)
    returned = shift(row_grad, SEQ, -1)
    low = jnp.where(late, returned, row_grad)
    high = returned
    local_grad = jnp.concatenate([low, high]).astype(f32)
    frame_grad = (
        jnp.zeros((length, width), f32)
        .at[local_index]
        .add(jnp.where(valid[:, None], local_grad, 0.0))
    )
    conv_grad = frame_grad * silu_grad(conv_out)
    grad_wide = with_halo(conv_grad, half_width)
    kernel_term = [
        jnp.sum(conv_grad * wide32[offset : offset + length], axis=0)
        for offset in range(tap_count)
    ]
    transposed = jnp.zeros((length, width), f32)
    for offset in range(tap_count):
        begin = 2 * half_width - offset
        transposed = transposed + conv_kernel[offset] * grad_wide[begin : begin + length]
    grad_x = (frame_grad + transposed).astype(bf16)[None]

    small = jnp.stack(kernel_term + [gain_term])
    near = ("core", "utt")
    part = exchange(small.reshape(lax.axis_size(near), 8, -1), near)
    part = jnp.sum(part, axis=0)
    part = spread(part, ("y", "z"))
    part = jnp.sum(part, axis=0)
    me = lax.axis_index("utt")
    ring = [part] + [turn(part, "utt", by) for by in range(1, utts)]
    ring = jnp.stack(ring[::-1] * 2)
    ring = lax.dynamic_slice_in_dim(ring, utts - 1 - me, utts, 0)
    other = turn(ring, "core", 1)
    full = [jnp.where(core == 0, ring, other), jnp.where(core == 0, other, ring)]
    full = jnp.stack(full).reshape(small.shape)
    load = exchange(chip, "z")
    grad_weight_in, grad_weight_out = jnp.sum(load.astype(f32), axis=0)
    return (grad_x, grad_weight_in, grad_weight_out, full[:tap_count], full[tap_count])


def solution(mesh):
    utts = mesh.shape["utt"]
    fine = Mesh(mesh.devices.reshape(4, 8, 2, utts), ("y", "z", "core", "utt"))
    placed = (
        P("utt", SEQ, None),
        P("utt", SEQ, None),
        P(),
        P(),
        P(SEQ, "utt"),
        P(("utt",) + SEQ, None),
        P("utt", None),
        P("utt", SEQ),
    )
    return jax.shard_map(
        per_device,
        mesh=fine,
        in_specs=placed,
        out_specs=(P("utt", SEQ, None), P(SEQ, "utt"), P(("utt",) + SEQ, None), P(), P()),
        check_vma=False,
    )
```

```python
import jax
import jax.numpy as jnp
from jax import lax
from jax.experimental.layout import Layout, with_layout_constraint
from jax.sharding import Mesh, PartitionSpec as P

norm_eps = 1e-05
BLOCK = 128
SEQ = ("y", "z", "core")
f32 = jnp.float32
bf16 = jnp.bfloat16


def shift(cells, axis, by):
    count = lax.axis_size(axis)
    return lax.ppermute(cells, axis, [(i, i + by) for i in range(count) if 0 <= i + by < count])


def turn(cells, axis, by):
    count = lax.axis_size(axis)
    return lax.ppermute(cells, axis, [(i, (i + by) % count) for i in range(count)])


def with_halo(cells, width):
    head = cells[:width]
    tail = cells[cells.shape[0] - width :]
    return jnp.concatenate([shift(tail, SEQ, 1), cells, shift(head, SEQ, -1)], axis=0)


def exchange(cells, axis):
    return lax.all_to_all(cells, axis, 0, 0, tiled=True)


def spread(cells, axis):
    count = lax.axis_size(axis)
    return exchange(jnp.broadcast_to(cells[None], (count,) + cells.shape), axis)


def pick(cells, which, axis):
    return lax.dynamic_index_in_dim(cells, which, axis, keepdims=False)


def pick_one(cells, flags):
    chosen = cells[0]
    for cell, flag in zip(cells[1:], flags[1:]):
        chosen = jnp.where(flag, cell, chosen)
    return chosen


def gather_weights(pair, core):
    half = spread(pair, "z")
    half = spread(half, "y")
    half = with_layout_constraint(half, Layout(major_to_minor=(0, 1, 2, 3, 4)))
    other = turn(half, "core", 1)
    width = pair.shape[-1]
    whole = []
    for i in range(2):
        ours, came = half[:, :, i], other[:, :, i]
        both = [jnp.where(core == 0, ours, came), jnp.where(core == 0, came, ours)]
        whole.append(jnp.stack(both, axis=2).reshape(-1, width))
    return whole


def scatter_grads(grads, core, rows):
    ny, nz = lax.axis_size("y"), lax.axis_size("z")
    cells = [g.reshape(ny, nz, 2, rows, g.shape[1]) for g in grads]
    theirs = jnp.concatenate([pick(c, 1 - core, 2) for c in cells], axis=1)
    mine = jnp.concatenate([pick(c, core, 2) for c in cells], axis=1)
    came = turn(theirs, "core", 1)
    chip = (mine.astype(f32) + came.astype(f32)).astype(bf16)
    spot = lax.axis_index("y")
    leave = [pick(chip, (spot + by) % ny, 0) for by in range(ny)]
    came = [turn(leave[by], "y", by) for by in range(1, ny)]
    chip = leave[0].astype(f32)
    for part in came:
        chip = chip + part.astype(f32)
    return chip.astype(bf16).reshape((2, nz) + chip.shape[1:]).transpose(1, 0, 2, 3)


def silu_grad(values):
    sigmoid = jax.nn.sigmoid(values)
    return sigmoid * (1.0 + values * (1.0 - sigmoid))


def per_device(
    features, cotangent, conv_kernel, norm_gain, weight_in, weight_out, keep_count, keep_index
):
    frames = features[0]
    length, width = frames.shape
    tap_count = conv_kernel.shape[0]
    half_width = tap_count // 2
    shard = lax.axis_index(SEQ)
    core = lax.axis_index("core")
    rows_in = weight_in.shape[0]

    w_in, w_out = gather_weights(jnp.stack([weight_in, weight_out]), core)

    counts = keep_count[0]
    blocks = (counts + BLOCK - 1) // BLOCK
    before = jnp.sum(jnp.where(jnp.arange(counts.shape[0]) < shard, blocks, 0))
    late = before - shard > 0
    local_index = keep_index[0]
    valid = jnp.arange(length, dtype=jnp.int32) < counts[shard]
    slots = jnp.arange(length, dtype=jnp.int32)
    chosen = ((local_index[:, None] == slots[None, :]) & valid[:, None]).astype(bf16)

    def place(rows):
        going = jnp.where(late, rows[:, :BLOCK], rows[:, BLOCK:])
        came = shift(going, SEQ, 1)
        return jnp.where(late, came, rows[:, :BLOCK])

    wide_rows = with_halo(frames, half_width)
    wide32 = wide_rows.astype(f32)
    conv_out = jnp.zeros((length, width), f32)
    for offset in range(tap_count):
        conv_out = conv_out + conv_kernel[offset] * wide32[offset : offset + length]
    hidden = (frames.astype(f32) + jax.nn.silu(conv_out)).astype(bf16)
    kept = jnp.stack(
        [
            jnp.dot(chosen, rows, preferred_element_type=f32).astype(bf16)
            for rows in (hidden, cotangent[0])
        ]
    )
    picked, picked_grad = place(kept)
    rows32 = picked.astype(f32)
    row_mean = jnp.mean(rows32, axis=1, keepdims=True)
    centred = rows32 - row_mean
    row_var = jnp.mean(centred * centred, axis=1, keepdims=True)
    inv_scale = lax.rsqrt(row_var + norm_eps)
    normed = centred * inv_scale
    scaled = (normed * norm_gain).astype(bf16)
    payload = jnp.stack([scaled, picked_grad])
    utts = lax.axis_size("utt")
    arrived = [payload] + [turn(payload, "utt", by) for by in range(1, utts)]
    scaled_all, grad_all = (jnp.concatenate([a[i] for a in arrived]) for i in range(2))
    plain = Layout(major_to_minor=(0, 1))
    grad_all = with_layout_constraint(grad_all, plain)

    pre_act = jnp.dot(scaled_all, w_in, preferred_element_type=f32)
    activation = jax.nn.silu(pre_act).astype(bf16)
    act_grad = 0.5 * lax.dot_general(
        grad_all, w_out, (((1,), (1,)), ((), ())), preferred_element_type=f32
    )
    up_grad = (act_grad * silu_grad(pre_act)).astype(bf16)
    partial_grad = lax.dot_general(
        up_grad, w_in, (((1,), (1,)), ((), ())), preferred_element_type=f32
    )
    parts = partial_grad.reshape(utts, BLOCK, width)
    norm_grad = parts[0]
    owed = [turn(parts[by].astype(bf16), "utt", -by) for by in range(1, utts)]
    for part in owed:
        norm_grad = norm_grad + part.astype(f32)

    over_rows = (((0,), (0,)), ((), ()))
    g_out = 0.5 * lax.dot_general(activation, grad_all, over_rows, preferred_element_type=f32)
    g_in = lax.dot_general(scaled_all, up_grad, over_rows, preferred_element_type=f32)
    g_out, g_in = g_out.astype(bf16), g_in.astype(bf16)
    chip = scatter_grads([g_in, g_out], core, rows_in)

    gain_term = jnp.sum(norm_grad * normed, axis=0)
    gain_grad = norm_grad * norm_gain
    back_term = (
        gain_grad
        - jnp.mean(gain_grad, axis=1, keepdims=True)
        - normed * jnp.mean(gain_grad * normed, axis=1, keepdims=True)
    ) * inv_scale
    row_grad = (picked_grad.astype(f32) + back_term).astype(bf16)
    returned = shift(row_grad, SEQ, -1)
    low = jnp.where(late, returned, row_grad)
    high = returned
    frame_grad = lax.dot_general(
        chosen,
        jnp.concatenate([low, high]),
        (((0,), (0,)), ((), ())),
        preferred_element_type=f32,
    )
    conv_grad = frame_grad * silu_grad(conv_out)
    grad_wide = with_halo(conv_grad, half_width)
    kernel_term = [
        jnp.sum(conv_grad * wide32[offset : offset + length], axis=0)
        for offset in range(tap_count)
    ]
    transposed = jnp.zeros((length, width), f32)
    for offset in range(tap_count):
        begin = 2 * half_width - offset
        transposed = transposed + conv_kernel[offset] * grad_wide[begin : begin + length]
    grad_x = (frame_grad + transposed).astype(bf16)[None]

    small = jnp.stack(kernel_term + [gain_term])
    near = ("core", "utt")
    part = exchange(small.reshape(lax.axis_size(near), 8, -1), near)
    part = jnp.sum(part, axis=0)
    part = spread(part, ("y", "z"))
    part = jnp.sum(part, axis=0)
    me = lax.axis_index("utt")
    ring = [part] + [turn(part, "utt", by) for by in range(1, utts)]
    ring = jnp.stack(
        [pick_one(ring, [(me - j) % utts == k for k in range(utts)]) for j in range(utts)]
    )
    other = turn(ring, "core", 1)
    full = [jnp.where(core == 0, ring, other), jnp.where(core == 0, other, ring)]
    full = jnp.stack(full).reshape(small.shape)
    load = exchange(chip, "z")
    grad_weight_in, grad_weight_out = jnp.sum(load.astype(f32), axis=0)
    return (grad_x, grad_weight_in, grad_weight_out, full[:tap_count], full[tap_count])


def solution(mesh):
    utts = mesh.shape["utt"]
    fine = Mesh(mesh.devices.reshape(4, 8, 2, utts), ("y", "z", "core", "utt"))
    placed = (
        P("utt", SEQ, None),
        P("utt", SEQ, None),
        P(),
        P(),
        P(SEQ, "utt"),
        P(("utt",) + SEQ, None),
        P("utt", None),
        P("utt", SEQ),
    )
    return jax.shard_map(
        per_device,
        mesh=fine,
        in_specs=placed,
        out_specs=(P("utt", SEQ, None), P(SEQ, "utt"), P(("utt",) + SEQ, None), P(), P()),
        check_vma=False,
    )
```
